512 devices in a mesh: tile: 64 (over z_lo, y, core), pgroup: 8 (over x, z_hi).
Axes of the slice: x: 4, y: 4, z: 16 (z_hi: 2, z_lo: 8; z = z_hi * 8 + z_lo), core: 2. Of those that a mesh axis runs over, the one named last changes fastest.
Arguments:
- echoes: bfloat16 [32768, 2, 4096], P(('pgroup', 'tile')), may hold values from -6 to 6
- offsets: int32 [64, 32768], P('tile', 'pgroup'), may hold values from 0 to 2041
- phase_index: int32 [64, 32768], P('tile', 'pgroup'), may hold values from 0 to 15
- steering: float32 [2, 64, 32768], P(None, 'tile'), may hold values from -2 to 2
- kernels: float32 [16, 8], replicated, may hold values from -2 to 2
Outputs:
- image: float32 [2, 2048, 16384], P(None, 'pgroup', 'tile')
The draws below stay inside these ranges and needn't reach their ends.
All inputs are finite; a program needn't handle non-finite values.
Results may differ from the reference program's by a relative error of at most 0.0037.
Values may be sent and summed in bfloat16 or wider, within the bound.
A program may use at most 64 MiB of HBM per device.

```python
import jax
import jax.numpy as jnp
from jax import lax

ROW_DEV = 256
COL_DEV = 256
PULSE_DEV = 64
R = 4096
TAPS = 8
PHASES = 16
STEPS = 4
TILES = 64
ROWS = 2048
COLS = 16384
PULSES = 32768
N_PGROUP = 8


def touch_ends(drawn, own_key, smallest, top_value):
    longest = drawn.shape.index(max(drawn.shape))
    spots = []
    for shift in (0, 1):
        where = [jax.random.randint(jax.random.fold_in(own_key, axis), (), 0, length) for axis, length in enumerate(drawn.shape)]
        where[longest] = (where[longest] + shift) % drawn.shape[longest]
        spots.append(tuple(where))
    return drawn.at[spots[0]].set(smallest).at[spots[1]].set(top_value)


def levels(key, extent, shards, low, high):
    def one(position, parts):
        draws = jax.random.uniform(jax.random.fold_in(jax.random.fold_in(key, 6), position), (parts,), jnp.float32, low / len(shards), high / len(shards))
        return jnp.repeat(jnp.exp(draws), extent[position] // parts).reshape((-1,) + (1,) * (len(extent) - position - 1))

    gain = one(*shards[0])
    for cut in shards[1:]:
        gain = gain * one(*cut)
    return gain


def noise(rng, shape, width, limit, cuts=(), kind=jnp.bfloat16):
    drawn = width * jax.random.normal(rng, shape, jnp.float32)
    if cuts:
        drawn = drawn * levels(rng, shape, cuts, -0.22, 0.18)
    return jnp.clip(drawn, -limit, limit).astype(kind)


def setup_inputs(seed: int = 0) -> dict:
    seeds = jax.random.split(jax.random.key(seed), 6)
    return {
        "echoes": noise(seeds[0], (PULSES, 2, R), 1.0, 6.0, ((0, 512),)),
        "offsets": touch_ends(jax.random.randint(seeds[1], (TILES, PULSES), 0, R - ROW_DEV * N_PGROUP - TAPS + 2), jax.random.fold_in(seeds[1], 1), 0, (R - ROW_DEV * N_PGROUP - TAPS + 2) - 1).astype(jnp.int32),
        "phase_index": touch_ends(jax.random.randint(seeds[2], (TILES, PULSES), 0, PHASES), jax.random.fold_in(seeds[2], 1), 0, PHASES - 1).astype(jnp.int32),
        "steering": jnp.clip(jax.random.uniform(seeds[3], (2, TILES, PULSES), jnp.float32, -2.0, 2.0) * levels(seeds[3], (2, TILES, PULSES), ((1, 64),), -0.4, 0.0), -2.0, 2.0),
        "kernels": noise(seeds[4], (PHASES, TAPS), TAPS ** -0.5, 2.0, (), jnp.float32),
    }


def steer_table(rates, curves, columns):
    centred = jnp.arange(columns, dtype=jnp.float32) - (columns - 1) / 2.0
    angle = rates[:, None] * centred[None, :] + curves[:, None] * (centred * centred / columns)[None, :]
    return jnp.cos(angle).astype(jnp.bfloat16), jnp.sin(angle).astype(jnp.bfloat16)


def reference(echoes, offsets, phase_index, steering, kernels):
    span = ROWS + TAPS - 1
    normaliser = (STEPS * PULSE_DEV * N_PGROUP) ** -0.5

    def one_tile(tile_at):
        behind = jnp.arange(STEPS, dtype=jnp.int32)
        group_ids = jnp.arange(N_PGROUP, dtype=jnp.int32)
        blocks = group_ids[:, None] * TILES + (tile_at - behind[None, :]) % TILES
        pulse_ids = (blocks[:, :, None] * PULSE_DEV + jnp.arange(PULSE_DEV, dtype=jnp.int32)[None, None, :]).reshape(-1)
        pulse_rows = echoes[pulse_ids]
        firsts = offsets[tile_at, pulse_ids].astype(jnp.int32)
        window = jax.vmap(lambda series, first: lax.dynamic_slice_in_dim(series, first, span, 1))(pulse_rows, firsts)
        weights = kernels[phase_index[tile_at, pulse_ids]]
        summed_taps = jnp.zeros((pulse_ids.shape[0], 2, ROWS), jnp.float32)
        for tap_index in range(TAPS):
            summed_taps = summed_taps + weights[:, tap_index, None, None] * window[:, :, tap_index:tap_index + ROWS].astype(jnp.float32)
        profile = summed_taps.astype(jnp.bfloat16)
        cosine, sine = steer_table(steering[0, tile_at, pulse_ids], steering[1, tile_at, pulse_ids], COL_DEV)
        real_part = jnp.dot(profile[:, 0].T, cosine, preferred_element_type=jnp.float32) - jnp.dot(profile[:, 1].T, sine, preferred_element_type=jnp.float32)
        imag_part = jnp.dot(profile[:, 0].T, sine, preferred_element_type=jnp.float32) + jnp.dot(profile[:, 1].T, cosine, preferred_element_type=jnp.float32)
        return jnp.stack([real_part, imag_part]) * normaliser

    per_tile = lax.map(one_tile, jnp.arange(TILES, dtype=jnp.int32))
    return jnp.transpose(per_tile, (1, 2, 0, 3)).reshape(2, ROWS, COLS)
```

```python
import functools

import jax
import jax.numpy as jnp
from jax import lax
from jax.experimental import pallas as pl
from jax.experimental.pallas import tpu as pltpu
from jax.sharding import PartitionSpec as P

MESH = pl.DeviceIdType.MESH
LANES = 128
STEPS = 4
TAPS = 8
TILES = 64
XS = 4
PULSES = 64
COLS = 256
WIDE = 2 * PULSES
SLOTS = STEPS * XS
PIECES = 4
ROW_BLOCKS = 16
BLOCKS_IN = 32


def profile_kernel(echo_ref, table_ref, out_ref):
    lane = lax.broadcasted_iota(jnp.int32, (16, LANES), 1)

    def step(i, carry):
        d = i // 8
        q = i // 4 % 2
        part = i % 4
        row = pl.multiple_of(q * PULSES + part * 16, 16)
        trow = pl.multiple_of(d * PULSES + part * 16, 16)
        table = table_ref[pl.ds(trow, 16), :]
        first = jnp.broadcast_to(table[:, 0:1], (16, LANES)).astype(jnp.int32)
        weights = [jnp.broadcast_to(table[:, 1 + j : 2 + j], (16, LANES)) for j in range(TAPS)]
        fine = first % LANES
        index = (lane + fine) % LANES
        inside = lane + fine < LANES
        coarse = first // LANES
        bits = [(coarse >> level) % 2 == 1 for level in range(4)]
        memo = {}

        def once(f):
            def g(*key):
                k = (f.__name__,) + key
                if k not in memo:
                    memo[k] = f(*key)
                return memo[k]

            return g

        @once
        def loaded(s):
            s = min(s, BLOCKS_IN - 1)
            return echo_ref[pl.ds(row, 16), s * LANES : (s + 1) * LANES].astype(jnp.float32)

        @once
        def chosen(level, s):
            if level == 4:
                return loaded(s)
            return jnp.where(bits[level], chosen(level + 1, s + (1 << level)), chosen(level + 1, s))

        @once
        def turned(s):
            return jnp.take_along_axis(chosen(0, s), index, axis=1)

        @once
        def window(s):
            return jnp.where(inside, turned(s), turned(s + 1))

        @once
        def rolled(name, s, by):
            return pltpu.roll(makers[name](s), LANES - by, 1)

        def moved(name, s, by):
            if s == ROW_BLOCKS:
                return rolled(name, s, by)
            return jnp.where(lane < LANES - by, rolled(name, s, by), rolled(name, s + 1, by))

        @once
        def next_one(s):
            return moved("w", s, 1)

        @once
        def pair(m, s):
            return weights[2 * m] * window(s) + weights[2 * m + 1] * next_one(s)

        @once
        def quad(m, s):
            return pair(2 * m, s) + moved("p%d" % (2 * m + 1), s, 2)

        makers = {
            "w": window,
            "p1": functools.partial(pair, 1),
            "p3": functools.partial(pair, 3),
            "q1": functools.partial(quad, 1),
        }
        for s in range(ROW_BLOCKS):
            value = quad(0, s) + moved("q1", s, 4)
            out_ref[d * ROW_BLOCKS + s, pl.ds(row, 16), :] = value.astype(jnp.bfloat16)
        return carry

    lax.fori_loop(0, 8 * STEPS, step, 0)


def tables(rates, curves):
    v = lax.broadcasted_iota(jnp.int32, (COLS, LANES), 0).astype(jnp.float32) - (COLS - 1) / 2.0
    angle = rates * v + curves * (v * v / COLS)
    turn = jnp.floor(angle * 0.6366197723675814 + 0.5)
    r = angle - turn * 1.5703125
    r = r - turn * 4.837512969970703125e-4
    r = r - turn * 7.54978995489188216e-8
    z = r * r
    s = ((-1.9515295891e-4 * z + 8.3321608736e-3) * z - 1.6666654611e-1) * z * r + r
    c = ((2.443315711809948e-5 * z - 1.388731625493765e-3) * z + 4.166664568298827e-2) * z * z - 0.5 * z + 1.0
    half = lax.broadcasted_iota(jnp.int32, (COLS, LANES), 1) // PULSES
    quarter = turn.astype(jnp.int32) + half
    odd = (quarter & 1) == 1
    first = jnp.where(odd, s, c)
    second = jnp.where(odd, c, s)
    first = jnp.where(((quarter + 1) & 2) == 2, -first, first)
    second = jnp.where((quarter & 2) == 2, -second, second)
    return first.astype(jnp.bfloat16), second.astype(jnp.bfloat16)


def exchange_kernel(scale, prof_ref, steer_ref, out_ref, held, left, zsend, zheld, own, ssem, rsem, zssem, zrsem):
    t = lax.axis_index("tile")
    g = lax.axis_index("pgroup")
    x = g // 2
    zh = g % 2
    here = zh * TILES + t

    def place(n, sign):
        d = n // XS
        rel = n % XS
        other = (here + sign * d + 2 * TILES) % (2 * TILES)
        return other % TILES, (x + sign * rel + XS) % XS * 2 + other // TILES, other // TILES

    barrier = pltpu.get_barrier_semaphore()

    def greet(n, carry):
        pt, pg, _ = place(n, -1)
        pl.semaphore_signal(barrier, inc=1, device_id=(pt, pg), device_id_type=MESH)
        return carry

    lax.fori_loop(1, SLOTS, greet, 0)
    pl.semaphore_signal(barrier, inc=1, device_id=(t, x * 2 + 1 - zh), device_id_type=MESH)

    def steer(n, carry):
        d = n // XS
        rel = n % XS
        source = (here - d + 2 * TILES) % (2 * TILES)
        sg = (x + XS - rel) % XS * 2 + source // TILES
        line = sg * TILES + source % TILES
        re, im = tables(steer_ref[pl.ds(line, 1), :], steer_ref[pl.ds(8 * TILES + line, 1), :])
        at = pl.ds(pl.multiple_of(n * WIDE, WIDE), WIDE)
        left[0:COLS, at] = re
        left[COLS : 2 * COLS, at] = im
        return carry

    lax.fori_loop(0, SLOTS, steer, 0)
    pl.semaphore_wait(barrier, SLOTS)

    def chunk(j, px, ph):
        half = jnp.where(j < 2, 1 - ph, ph)
        return px * 4 + half * 2 + j % 2

    def send(j, n):
        pt, pg, ph = place(n, 1)
        d = n // XS
        return pltpu.make_async_remote_copy(
            src_ref=prof_ref.at[d * ROW_BLOCKS + chunk(j, pg // 2, ph)],
            dst_ref=held.at[j, pl.ds(pl.multiple_of(n * WIDE, WIDE), WIDE)],
            send_sem=ssem.at[j, n],
            recv_sem=rsem.at[j, n],
            device_id=(pt, pg),
            device_id_type=MESH,
        )

    def start_all(i, carry):
        send(i // (SLOTS - 1), i % (SLOTS - 1) + 1).start()
        return carry

    lax.fori_loop(0, PIECES * (SLOTS - 1), start_all, 0)

    def take(j, carry):
        held[j, 0:WIDE, :] = prof_ref[chunk(j, x, zh)]
        return carry

    lax.fori_loop(0, PIECES, take, 0)

    def arrived(j):
        def one(n, carry):
            send(j, n).wait_recv()
            return carry

        lax.fori_loop(1, SLOTS, one, 0)
        return jnp.dot(left[...], held[j], preferred_element_type=jnp.float32)

    def across(j):
        return pltpu.make_async_remote_copy(
            src_ref=zsend.at[j],
            dst_ref=zheld.at[j],
            send_sem=zssem.at[j],
            recv_sem=zrsem.at[j],
            device_id=(t, x * 2 + 1 - zh),
            device_id_type=MESH,
        )

    def far(j, carry):
        zsend[j] = arrived(j).astype(jnp.bfloat16)
        across(j).start()
        return carry

    def near(j, carry):
        own[j] = arrived(j + 2)
        return carry

    def finish(j, carry):
        across(j).wait_recv()
        total = (own[j] + zheld[j].astype(jnp.float32)) * scale
        rows = pl.ds(pl.multiple_of(j * LANES, LANES), LANES)
        out_ref[0, rows, :] = total[0:COLS].T
        out_ref[1, rows, :] = total[COLS : 2 * COLS].T
        return carry

    def drain(i, carry):
        send(i // (SLOTS - 1), i % (SLOTS - 1) + 1).wait_send()
        return carry

    lax.fori_loop(0, 2, far, 0)
    lax.fori_loop(0, 2, near, 0)
    lax.fori_loop(0, 2, finish, 0)
    lax.fori_loop(0, PIECES * (SLOTS - 1), drain, 0)
    across(0).wait_send()
    across(1).wait_send()


def per_device(echoes, offsets, phase_index, steering, kernels):
    t = lax.axis_index("tile")
    scale = (STEPS * PULSES * lax.axis_size("pgroup")) ** (-0.5)
    vmem = pl.BlockSpec(memory_space=pltpu.VMEM)

    def near(a):
        blocks = a.reshape(TILES, PULSES)
        return lax.dynamic_slice_in_dim(jnp.concatenate([blocks[TILES - 3 :], blocks]), t, STEPS)[::-1]

    firsts = near(offsets).astype(jnp.float32)
    phases = near(phase_index)
    onehot = (phases[:, :, None] == jnp.arange(kernels.shape[0], dtype=jnp.int32)).astype(jnp.float32)
    weights = jnp.dot(onehot, kernels, precision=lax.Precision.HIGHEST)
    table = jnp.concatenate([firsts[:, :, None], weights], 2)
    table = jnp.pad(table, ((0, 0), (0, 0), (0, LANES - 1 - TAPS)))
    sent = [table[0]]
    for d in range(1, STEPS):
        sent.append(lax.ppermute(table[d], "tile", [(i, (i - d) % TILES) for i in range(TILES)]))
    table = jnp.concatenate(sent)
    rows = jnp.transpose(echoes, (1, 0, 2)).reshape(WIDE, echoes.shape[2])
    profile = pl.pallas_call(
        profile_kernel,
        out_shape=jax.ShapeDtypeStruct((STEPS * ROW_BLOCKS, WIDE, LANES), jnp.bfloat16),
        in_specs=[vmem, vmem],
        out_specs=vmem,
    )(rows, table)
    steer = steering.reshape(-1, PULSES)
    steer = jnp.concatenate([steer, steer], 1)
    return pl.pallas_call(
        functools.partial(exchange_kernel, scale),
        out_shape=jax.ShapeDtypeStruct((2, COLS, COLS), jnp.float32),
        in_specs=[vmem, vmem],
        out_specs=vmem,
        scratch_shapes=[
            pltpu.VMEM((PIECES, SLOTS * WIDE, LANES), jnp.bfloat16),
            pltpu.VMEM((2 * COLS, SLOTS * WIDE), jnp.bfloat16),
            pltpu.VMEM((2, 2 * COLS, LANES), jnp.bfloat16),
            pltpu.VMEM((2, 2 * COLS, LANES), jnp.bfloat16),
            pltpu.VMEM((2, 2 * COLS, LANES), jnp.float32),
            pltpu.SemaphoreType.DMA((PIECES, SLOTS)),
            pltpu.SemaphoreType.DMA((PIECES, SLOTS)),
            pltpu.SemaphoreType.DMA((2,)),
            pltpu.SemaphoreType.DMA((2,)),
        ],
        compiler_params=pltpu.CompilerParams(collective_id=0, has_side_effects=True),
    )(profile, steer)


def solution(mesh):
    placed = (
        P(("pgroup", "tile"), None, None),
        P("tile", "pgroup"),
        P("tile", "pgroup"),
        P(None, "tile", None),
        P(),
    )
    return jax.shard_map(
        per_device, mesh=mesh, in_specs=placed, out_specs=P(None, "pgroup", "tile"), check_vma=False
    )
```

```python
import functools

import jax
import jax.numpy as jnp
from jax import lax
from jax.experimental import pallas as pl
from jax.experimental.pallas import tpu as pltpu
from jax.sharding import PartitionSpec as P

MESH = pl.DeviceIdType.MESH
LANES = 128
STEPS = 4
TAPS = 8
TILES = 64
XS = 4
PULSES = 64
COLS = 256
WIDE = 2 * PULSES
SLOTS = STEPS * XS
PIECES = 4
ROW_BLOCKS = 16
BLOCKS_IN = 32
SIN = (6.2831853, -41.3417004, 81.6051314, -76.7030154, 42.025927, -14.8998467, 3.23813751)
COS = (1, -19.7392087, 64.9393891, -85.4566583, 60.2421313, -26.4046682, 7.80013142, -1.45311229)


def build_profile(echo_ref, table_ref, out_ref, d, part):
    lane = lax.broadcasted_iota(jnp.int32, (16, LANES), 1)
    trow = pl.multiple_of(d * PULSES + part * 16, 16)
    table = table_ref[pl.ds(trow, 16), :]
    first = jnp.broadcast_to(table[:, TAPS : TAPS + 1], (16, LANES)).astype(jnp.int32)
    weights = [jnp.broadcast_to(table[:, j : 1 + j], (16, LANES)) for j in range(TAPS)]
    fine = first & (LANES - 1)
    ahead = lane + fine
    index = ahead & (LANES - 1)
    inside = ahead < LANES
    bits = []
    for level in range(4):
        on = (first >> (7 + level)) & 1
        bits.append(on.astype(jnp.float32).astype(jnp.bfloat16) > 0.5)
    for q in range(2):
        row = pl.multiple_of(q * PULSES + part * 16, 16)
        memo = {}

        def once(f, memo=memo):
            def g(*key):
                k = (f.__name__,) + key
                if k not in memo:
                    memo[k] = f(*key)
                return memo[k]

            return g

        @once
        def loaded(s, row=row):
            s = min(s, BLOCKS_IN - 1)
            return echo_ref[pl.ds(row, 16), s * LANES : (s + 1) * LANES]

        @once
        def chosen(level, s):
            if level == 4:
                return loaded(s)
            return jnp.where(bits[level], chosen(level + 1, s + (1 << level)), chosen(level + 1, s))

        @once
        def turned(s):
            return jnp.take_along_axis(chosen(0, s).astype(jnp.float32), index, axis=1)

        @once
        def window(s):
            return jnp.where(inside, turned(s), turned(s + 1))

        @once
        def rolled(name, s, by):
            return pltpu.roll(makers[name](s), LANES - by, 1)

        def moved(name, s, by):
            if s == ROW_BLOCKS:
                return rolled(name, s, by)
            return jnp.where(lane < LANES - by, rolled(name, s, by), rolled(name, s + 1, by))

        @once
        def next_one(s):
            return moved("w", s, 1)

        @once
        def pair(m, s):
            return weights[2 * m] * window(s) + weights[2 * m + 1] * next_one(s)

        @once
        def quad(m, s):
            return pair(2 * m, s) + moved("p%d" % (2 * m + 1), s, 2)

        makers = {
            "w": window,
            "p1": functools.partial(pair, 1),
            "p3": functools.partial(pair, 3),
            "q1": functools.partial(quad, 1),
        }
        for s in range(ROW_BLOCKS):
            value = quad(0, s) + moved("q1", s, 4)
            out_ref[d * ROW_BLOCKS + s, pl.ds(row, 16), :] = value.astype(jnp.bfloat16)


def half_row(ref, block, *lead):
    at = pl.ds(pl.multiple_of(block // 2 * LANES, LANES), LANES)
    row = ref[(*lead, slice(None), at)] if lead else ref[:, at]
    return jnp.where(block % 2 == 1, pltpu.roll(row, PULSES, 1), row)


def tables(rates, curves, phase):
    v = lax.broadcasted_iota(jnp.int32, (COLS, LANES), 0).astype(jnp.float32) - (COLS - 1) / 2.0
    turns = rates * v + curves * (v * v * (1.0 / COLS)) + phase
    whole = (turns + 12582912.0) - 12582912.0
    f = turns - whole
    z = f * f
    s = SIN[-1]
    for k in SIN[-2::-1]:
        s = s * z + k
    s = s * f
    c = COS[-1]
    for k in COS[-2::-1]:
        c = c * z + k
    return c.astype(jnp.bfloat16), s.astype(jnp.bfloat16)


def strip_kernel(
    scale, echo_ref, offs_ref, phase_ref, steer_ref, kern_ref, out_ref,
    prof, tab, tsend, kpad, held, left, zsend, zheld, own, tssem, trsem, ssem, rsem, zssem, zrsem,
):
    t = lax.axis_index("tile")
    g = lax.axis_index("pgroup")
    x = g // 2
    zh = g % 2
    here = zh * TILES + t

    def place(n, sign):
        d = n // XS
        rel = n % XS
        other = (here + sign * d + 2 * TILES) % (2 * TILES)
        return other % TILES, (x + sign * rel + XS) % XS * 2 + other // TILES, other // TILES

    barrier = pltpu.get_barrier_semaphore()

    def greet(n, carry):
        pt, pg, _ = place(n, -1)
        pl.semaphore_signal(barrier, inc=1, device_id=(pt, pg), device_id_type=MESH)
        return carry

    lax.fori_loop(1, SLOTS, greet, 0)
    pl.semaphore_signal(barrier, inc=1, device_id=(t, x * 2 + 1 - zh), device_id_type=MESH)
    for d in range(1, STEPS):
        pl.semaphore_signal(barrier, inc=1, device_id=((t + d) % TILES, g), device_id_type=MESH)

    kpad[...] = jnp.zeros_like(kpad)
    kpad[0 : kern_ref.shape[0], 0:TAPS] = kern_ref[...]
    lane = lax.broadcasted_iota(jnp.int32, (PULSES, LANES), 1)
    eye = lane == lax.broadcasted_iota(jnp.int32, (PULSES, LANES), 0)

    def window_table(d):
        block = (t + TILES - d) % TILES
        firsts = half_row(offs_ref, block).astype(jnp.float32)
        phases = half_row(phase_ref, block).astype(jnp.float32)
        first = jnp.sum(jnp.where(eye, firsts, 0.0), axis=1, keepdims=True)
        kind = jnp.sum(jnp.where(eye, phases, 0.0), axis=1, keepdims=True)
        onehot = jnp.where(lane.astype(jnp.float32) == kind, 1.0, 0.0)
        weights = jnp.dot(
            onehot, kpad[...], precision=lax.Precision.HIGHEST, preferred_element_type=jnp.float32
        )
        return jnp.where(lane == TAPS, first, weights)

    tab[0:PULSES] = window_table(0)
    for d in range(1, STEPS):
        tsend[d - 1] = window_table(d)

    def table_copy(d):
        return pltpu.make_async_remote_copy(
            src_ref=tsend.at[d - 1],
            dst_ref=tab.at[pl.ds(pl.multiple_of(d * PULSES, PULSES), PULSES)],
            send_sem=tssem.at[d],
            recv_sem=trsem.at[d],
            device_id=((t + TILES - d) % TILES, g),
            device_id_type=MESH,
        )

    lane_row = lax.broadcasted_iota(jnp.int32, (1, LANES), 1)
    quarter = jnp.where(lane_row < PULSES, 0.0, 0.25)

    def steer(n, carry):
        d = n // XS
        rel = n % XS
        source = (here - d + 2 * TILES) % (2 * TILES)
        sg = (x + XS - rel) % XS * 2 + source // TILES
        line = sg * TILES + source % TILES

        def both(i):
            row = half_row(steer_ref, line, i)
            return jnp.where(lane_row < PULSES, row, pltpu.roll(row, PULSES, 1)) * (0.5 / 3.141592653589793)

        re, im = tables(both(0), both(1), quarter)
        at = pl.ds(pl.multiple_of(n * WIDE, WIDE), WIDE)
        left[0:COLS, at] = re
        left[COLS : 2 * COLS, at] = im
        return carry

    lax.fori_loop(0, SLOTS, steer, 0)
    pl.semaphore_wait(barrier, SLOTS + STEPS - 1)
    for d in range(1, STEPS):
        table_copy(d).start()

    def chunk(j, px, ph):
        half = jnp.where(j < 2, 1 - ph, ph)
        return px * 4 + half * 2 + j % 2

    def send(j, n):
        pt, pg, ph = place(n, 1)
        d = n // XS
        return pltpu.make_async_remote_copy(
            src_ref=prof.at[d * ROW_BLOCKS + chunk(j, pg // 2, ph)],
            dst_ref=held.at[j, pl.ds(pl.multiple_of(n * WIDE, WIDE), WIDE)],
            send_sem=ssem.at[j, n],
            recv_sem=rsem.at[j, n],
            device_id=(pt, pg),
            device_id_type=MESH,
        )

    def distance(i, carry):
        d = (STEPS - i) % STEPS

        @pl.when(d > 0)
        def _():
            table_copy(d).wait_recv()

        def part(p, c):
            build_profile(echo_ref, tab, prof, d, p)
            return c

        lax.fori_loop(0, PULSES // 16, part, 0)

        def early(m, c):
            n = d * XS + m % XS

            @pl.when(n > 0)
            def _():
                send(m // XS, n).start()

            return c

        lax.fori_loop(0, 2 * XS, early, 0)
        return carry

    lax.fori_loop(0, STEPS, distance, 0)

    def late(i, carry):
        send(2 + i // (SLOTS - 1), i % (SLOTS - 1) + 1).start()
        return carry

    lax.fori_loop(0, 2 * (SLOTS - 1), late, 0)

    def take(j, carry):
        held[j, 0:WIDE, :] = prof[chunk(j, x, zh)]
        return carry

    lax.fori_loop(0, PIECES, take, 0)

    def arrived(j):
        def one(n, carry):
            send(j, n).wait_recv()
            return carry

        lax.fori_loop(1, SLOTS, one, 0)
        return jnp.dot(left[...], held[j], preferred_element_type=jnp.float32)

    def across(j):
        return pltpu.make_async_remote_copy(
            src_ref=zsend.at[j],
            dst_ref=zheld.at[j],
            send_sem=zssem.at[j],
            recv_sem=zrsem.at[j],
            device_id=(t, x * 2 + 1 - zh),
            device_id_type=MESH,
        )

    def far(j, carry):
        zsend[j] = arrived(j).astype(jnp.bfloat16)
        across(j).start()
        return carry

    def near(j, carry):
        own[j] = arrived(j + 2)
        return carry

    def finish(j, carry):
        across(j).wait_recv()
        total = (own[j] + zheld[j].astype(jnp.float32)) * scale
        rows = pl.ds(pl.multiple_of(j * LANES, LANES), LANES)
        out_ref[0, rows, :] = total[0:COLS].T
        out_ref[1, rows, :] = total[COLS : 2 * COLS].T
        return carry

    def drain(i, carry):
        send(i // (SLOTS - 1), i % (SLOTS - 1) + 1).wait_send()
        return carry

    lax.fori_loop(0, 2, far, 0)
    lax.fori_loop(0, 2, near, 0)
    lax.fori_loop(0, 2, finish, 0)
    lax.fori_loop(0, PIECES * (SLOTS - 1), drain, 0)
    for d in range(1, STEPS):
        table_copy(d).wait_send()
    across(0).wait_send()
    across(1).wait_send()


def per_device(echoes, offsets, phase_index, steering, kernels):
    scale = (STEPS * PULSES * lax.axis_size("pgroup")) ** (-0.5)
    vmem = pl.BlockSpec(memory_space=pltpu.VMEM)
    rows = jnp.transpose(echoes, (1, 0, 2)).reshape(WIDE, echoes.shape[2])
    dma = pltpu.SemaphoreType.DMA
    return pl.pallas_call(
        functools.partial(strip_kernel, scale),
        out_shape=jax.ShapeDtypeStruct((2, COLS, COLS), jnp.float32),
        in_specs=[vmem] * 5,
        out_specs=vmem,
        scratch_shapes=[
            pltpu.VMEM((STEPS * ROW_BLOCKS, WIDE, LANES), jnp.bfloat16),
            pltpu.VMEM((STEPS * PULSES, LANES), jnp.float32),
            pltpu.VMEM((STEPS - 1, PULSES, LANES), jnp.float32),
            pltpu.VMEM((LANES, LANES), jnp.float32),
            pltpu.VMEM((PIECES, SLOTS * WIDE, LANES), jnp.bfloat16),
            pltpu.VMEM((2 * COLS, SLOTS * WIDE), jnp.bfloat16),
            pltpu.VMEM((2, 2 * COLS, LANES), jnp.bfloat16),
            pltpu.VMEM((2, 2 * COLS, LANES), jnp.bfloat16),
            pltpu.VMEM((2, 2 * COLS, LANES), jnp.float32),
            dma((STEPS,)),
            dma((STEPS,)),
            dma((PIECES, SLOTS)),
            dma((PIECES, SLOTS)),
            dma((2,)),
            dma((2,)),
        ],
        compiler_params=pltpu.CompilerParams(collective_id=0, has_side_effects=True),
    )(rows, offsets, phase_index, steering, kernels)


def solution(mesh):
    placed = (
        P(("pgroup", "tile"), None, None),
        P("tile", "pgroup"),
        P("tile", "pgroup"),
        P(None, "tile", None),
        P(),
    )
    return jax.shard_map(
        per_device, mesh=mesh, in_specs=placed, out_specs=P(None, "pgroup", "tile"), check_vma=False
    )
```

```python
import functools

import jax
import jax.numpy as jnp
from jax import lax
from jax.experimental import pallas as pl
from jax.experimental.pallas import tpu as pltpu
from jax.sharding import PartitionSpec as P

MESH = pl.DeviceIdType.MESH
LANES = 128
STEPS = 4
TAPS = 8
TILES = 64
XS = 4
PULSES = 64
COLS = 256
WIDE = 2 * PULSES
SLOTS = STEPS * XS
PIECES = 4
LEG = 32
QUARTERS = 8
QROWS = 64
ROW_BLOCKS = 16
BLOCKS_IN = 32
SIN = (6.2831853, -41.3417004, 81.6051314, -76.7030154, 42.025927, -14.8998467, 3.23813751)
COS = (1, -19.7392087, 64.9393891, -85.4566583, 60.2421313, -26.4046682, 7.80013142, -1.45311229)


def build_profile(echo_ref, table_ref, out_ref, d, part):
    lane = lax.broadcasted_iota(jnp.int32, (16, LANES), 1)
    trow = pl.multiple_of(d * PULSES + part * 16, 16)
    table = table_ref[pl.ds(trow, 16), :]
    first = jnp.broadcast_to(table[:, TAPS : TAPS + 1], (16, LANES)).astype(jnp.int32)
    weights = [jnp.broadcast_to(table[:, j : 1 + j], (16, LANES)) for j in range(TAPS)]
    fine = first & (LANES - 1)
    ahead = lane + fine
    index = ahead & (LANES - 1)
    inside = ahead < LANES
    bits = []
    for level in range(4):
        on = (first >> (7 + level)) & 1
        bits.append(on.astype(jnp.float32).astype(jnp.bfloat16) > 0.5)
    for q in range(2):
        row = pl.multiple_of(q * PULSES + part * 16, 16)
        memo = {}

        def once(f, memo=memo):
            def g(*key):
                k = (f.__name__,) + key
                if k not in memo:
                    memo[k] = f(*key)
                return memo[k]

            return g

        @once
        def loaded(s, row=row):
            s = min(s, BLOCKS_IN - 1)
            return echo_ref[pl.ds(row, 16), s * LANES : (s + 1) * LANES]

        @once
        def chosen(level, s):
            if level == 4:
                return loaded(s)
            return jnp.where(bits[level], chosen(level + 1, s + (1 << level)), chosen(level + 1, s))

        @once
        def turned(s):
            return jnp.take_along_axis(chosen(0, s).astype(jnp.float32), index, axis=1)

        @once
        def window(s):
            return jnp.where(inside, turned(s), turned(s + 1))

        @once
        def rolled(name, s, by):
            return pltpu.roll(makers[name](s), LANES - by, 1)

        def moved(name, s, by):
            if s == ROW_BLOCKS:
                return rolled(name, s, by)
            return jnp.where(lane < LANES - by, rolled(name, s, by), rolled(name, s + 1, by))

        @once
        def next_one(s):
            return moved("w", s, 1)

        @once
        def pair(m, s):
            return weights[2 * m] * window(s) + weights[2 * m + 1] * next_one(s)

        @once
        def quad(m, s):
            return pair(2 * m, s) + moved("p%d" % (2 * m + 1), s, 2)

        makers = {
            "w": window,
            "p1": functools.partial(pair, 1),
            "p3": functools.partial(pair, 3),
            "q1": functools.partial(quad, 1),
        }
        for s in range(ROW_BLOCKS):
            value = quad(0, s) + moved("q1", s, 4)
            out_ref[d * ROW_BLOCKS + s, pl.ds(row, 16), :] = value.astype(jnp.bfloat16)


def half_row(ref, block, *lead):
    at = pl.ds(pl.multiple_of((block >> 1) * LANES, LANES), LANES)
    row = ref[(*lead, slice(None), at)] if lead else ref[:, at]
    return jnp.where((block & 1) == 1, pltpu.roll(row, PULSES, 1), row)


def tables(rates, curves, phase):
    v = lax.broadcasted_iota(jnp.int32, (COLS, LANES), 0).astype(jnp.float32) - (COLS - 1) / 2.0
    turns = rates * v + curves * (v * v * (1.0 / COLS)) + phase
    whole = (turns + 12582912.0) - 12582912.0
    f = turns - whole
    z = f * f
    s = SIN[-1]
    for k in SIN[-2::-1]:
        s = s * z + k
    s = s * f
    c = COS[-1]
    for k in COS[-2::-1]:
        c = c * z + k
    return c.astype(jnp.bfloat16), s.astype(jnp.bfloat16)


def strip_kernel(
    scale, echo_ref, offs_ref, phase_ref, steer_ref, kern_ref, out_ref,
    prof, tab, tsend, kpad, held, left, zsend, relay, zheld, own, tssem, trsem, ssem, rsem, zssem, zrsem,
):
    t = lax.axis_index("tile")
    g = lax.axis_index("pgroup")
    x = g >> 1
    zh = g & 1
    here = zh * TILES + t

    def place(n, sign):
        d = n >> 2
        rel = n & (XS - 1)
        other = (here + sign * d) & (2 * TILES - 1)
        return other & (TILES - 1), ((x + sign * rel) & (XS - 1)) * 2 + (other >> 6), other >> 6

    barrier = pltpu.get_barrier_semaphore()

    def greet(n, carry):
        pt, pg, _ = place(n, -1)
        pl.semaphore_signal(barrier, inc=1, device_id=(pt, pg), device_id_type=MESH)
        return carry

    lax.fori_loop(1, SLOTS, greet, 0)
    def along(by):
        other = (here + by) & (2 * TILES - 1)
        return other & (TILES - 1), x * 2 + (other >> 6)

    for by in (-LEG, LEG):
        pl.semaphore_signal(barrier, inc=1, device_id=along(by), device_id_type=MESH)
    for d in range(1, STEPS):
        pl.semaphore_signal(barrier, inc=1, device_id=((t + d) & (TILES - 1), g), device_id_type=MESH)

    kpad[...] = jnp.zeros_like(kpad)
    kpad[0:TAPS, 0 : kern_ref.shape[1]] = kern_ref[...]
    lane = lax.broadcasted_iota(jnp.int32, (PULSES, LANES), 1)
    eye = lane == lax.broadcasted_iota(jnp.int32, (PULSES, LANES), 0)

    def window_table(d):
        block = (t - d) & (TILES - 1)
        firsts = half_row(offs_ref, block).astype(jnp.float32)
        phases = half_row(phase_ref, block).astype(jnp.float32)
        first = jnp.sum(jnp.where(eye, firsts, 0.0), axis=1, keepdims=True)
        kind = jnp.sum(jnp.where(eye, phases, 0.0), axis=1, keepdims=True)
        onehot = jnp.where(lane.astype(jnp.float32) == kind, 1.0, 0.0)
        weights = lax.dot_general(
            onehot,
            kpad[...],
            (((1,), (1,)), ((), ())),
            precision=lax.Precision.HIGHEST,
            preferred_element_type=jnp.float32,
        )
        return jnp.where(lane == TAPS, first, weights)

    tab[0:PULSES] = window_table(0)
    for d in range(1, STEPS):
        tsend[d - 1] = window_table(d)

    def table_copy(d):
        return pltpu.make_async_remote_copy(
            src_ref=tsend.at[d - 1],
            dst_ref=tab.at[pl.ds(pl.multiple_of(d * PULSES, PULSES), PULSES)],
            send_sem=tssem.at[d],
            recv_sem=trsem.at[d],
            device_id=((t - d) & (TILES - 1), g),
            device_id_type=MESH,
        )

    lane_row = lax.broadcasted_iota(jnp.int32, (1, LANES), 1)
    quarter = jnp.where(lane_row < PULSES, 0.0, 0.25)

    def steer(n, carry):
        d = n >> 2
        rel = n & (XS - 1)
        source = (here - d) & (2 * TILES - 1)
        line = (((x - rel) & (XS - 1)) * 2 + (source >> 6)) * TILES + (source & (TILES - 1))

        def both(i):
            row = half_row(steer_ref, line, i)
            return jnp.where(lane_row < PULSES, row, pltpu.roll(row, PULSES, 1)) * (0.5 / 3.141592653589793)

        re, im = tables(both(0), both(1), quarter)
        at = pl.ds(pl.multiple_of(n * WIDE, WIDE), WIDE)
        left[0:COLS, at] = re
        left[COLS : 2 * COLS, at] = im
        return carry


    def chunk(j, px, ph):
        return px * 4 + (ph ^ 1 ^ (j >> 1)) * 2 + (j & 1)

    def send(j, n):
        pt, pg, ph = place(n, 1)
        return pltpu.make_async_remote_copy(
            src_ref=prof.at[(n >> 2) * ROW_BLOCKS + chunk(j, pg >> 1, ph)],
            dst_ref=held.at[j, pl.ds(pl.multiple_of(n * WIDE, WIDE), WIDE)],
            send_sem=ssem.at[j, n],
            recv_sem=rsem.at[j, n],
            device_id=(pt, pg),
            device_id_type=MESH,
        )

    def distance(i, carry):
        d = (STEPS - i) & (STEPS - 1)

        @pl.when(d > 0)
        def _():
            table_copy(d).wait_recv()

        def part(p, c):
            build_profile(echo_ref, tab, prof, d, p)
            return c

        lax.fori_loop(0, PULSES // 16, part, 0)

        @pl.when(d == 0)
        def _():
            pl.semaphore_wait(barrier, SLOTS + STEPS)
            for b in range(1, STEPS):
                table_copy(b).start()

        def early(j, c):
            for rel in range(XS):
                n = d * XS + rel
                if rel == 0:

                    @pl.when(d > 0)
                    def _():
                        send(j, n).start()

                else:
                    send(j, n).start()
            return c

        lax.fori_loop(0, 2, early, 0)
        return carry

    lax.fori_loop(0, STEPS, distance, 0)

    def late(n, carry):
        send(2, n).start()
        send(3, n).start()
        return carry

    def early_drain(n, carry):
        send(0, n).wait_send()
        send(1, n).wait_send()
        return carry

    lax.fori_loop(0, SLOTS, steer, 0)
    lax.fori_loop(1, SLOTS, early_drain, 0)
    lax.fori_loop(1, SLOTS, late, 0)

    def take(j, carry):
        held[j, 0:WIDE, :] = prof[chunk(j, x, zh)]
        return carry

    lax.fori_loop(0, PIECES, take, 0)

    def arrived(j):
        def one(n, carry):
            send(j, n).wait_recv()
            return carry

        lax.fori_loop(1, SLOTS, one, 0)
        return jnp.dot(left[...], held[j], preferred_element_type=jnp.float32)

    y = (t >> 1) & 3

    def leg(j, k, second):
        up = k < plus(y)
        rows = pl.ds(pl.multiple_of(k * QROWS, QROWS), QROWS)
        return pltpu.make_async_remote_copy(
            src_ref=(relay if second else zsend).at[j, rows],
            dst_ref=(zheld if second else relay).at[j, rows],
            send_sem=zssem.at[second, j, k],
            recv_sem=zrsem.at[second, j, k],
            device_id=along(jnp.where(up, LEG, -LEG)),
            device_id_type=MESH,
        )

    def far(j, carry):
        zsend[j] = arrived(j).astype(jnp.bfloat16)
        for k in range(QUARTERS):
            leg(j, k, 0).start()
        return carry

    def forward(j, carry):
        for k in range(QUARTERS):
            leg(j, k, 0).wait_recv()
            leg(j, k, 1).start()
        return carry

    def near(j, carry):
        own[j] = arrived(j + 2)
        return carry

    def finish(j, carry):
        for k in range(QUARTERS):
            leg(j, k, 1).wait_recv()
        out_ref[j] = (own[j] + zheld[j].astype(jnp.float32)) * scale
        return carry

    def late_drain(n, carry):
        send(2, n).wait_send()
        send(3, n).wait_send()
        return carry

    lax.fori_loop(0, 2, far, 0)
    lax.fori_loop(0, 2, forward, 0)
    lax.fori_loop(0, 2, near, 0)
    lax.fori_loop(0, 2, finish, 0)
    lax.fori_loop(1, SLOTS, late_drain, 0)
    for d in range(1, STEPS):
        table_copy(d).wait_send()
    for j in range(2):
        for k in range(QUARTERS):
            leg(j, k, 0).wait_send()
            leg(j, k, 1).wait_send()


def plus(y):
    return jnp.where(y == 3, 2, 4)


def turn_kernel(in_ref, out_ref):
    for j in range(2):
        for i in range(2):
            out_ref[i, j * LANES : (j + 1) * LANES, :] = in_ref[j, i * COLS : (i + 1) * COLS].T


def per_device(echoes, offsets, phase_index, steering, kernels):
    scale = (STEPS * PULSES * lax.axis_size("pgroup")) ** (-0.5)
    vmem = pl.BlockSpec(memory_space=pltpu.VMEM)
    rows = jnp.transpose(echoes, (1, 0, 2)).reshape(WIDE, echoes.shape[2])
    dma = pltpu.SemaphoreType.DMA
    total = pl.pallas_call(
        functools.partial(strip_kernel, scale),
        out_shape=jax.ShapeDtypeStruct((2, 2 * COLS, LANES), jnp.float32),
        in_specs=[vmem] * 5,
        out_specs=vmem,
        scratch_shapes=[
            pltpu.VMEM((STEPS * ROW_BLOCKS, WIDE, LANES), jnp.bfloat16),
            pltpu.VMEM((STEPS * PULSES, LANES), jnp.float32),
            pltpu.VMEM((STEPS - 1, PULSES, LANES), jnp.float32),
            pltpu.VMEM((LANES, LANES), jnp.float32),
            pltpu.VMEM((PIECES, SLOTS * WIDE, LANES), jnp.bfloat16),
            pltpu.VMEM((2 * COLS, SLOTS * WIDE), jnp.bfloat16),
            pltpu.VMEM((2, 2 * COLS, LANES), jnp.bfloat16),
            pltpu.VMEM((2, 2 * COLS, LANES), jnp.bfloat16),
            pltpu.VMEM((2, 2 * COLS, LANES), jnp.bfloat16),
            pltpu.VMEM((2, 2 * COLS, LANES), jnp.float32),
            dma((STEPS,)),
            dma((STEPS,)),
            dma((PIECES, SLOTS)),
            dma((PIECES, SLOTS)),
            dma((2, 2, QUARTERS)),
            dma((2, 2, QUARTERS)),
        ],
        compiler_params=pltpu.CompilerParams(collective_id=0, has_side_effects=True),
    )(rows, offsets, phase_index, steering, kernels.T)
    return pl.pallas_call(
        turn_kernel,
        out_shape=jax.ShapeDtypeStruct((2, COLS, COLS), jnp.float32),
        in_specs=[vmem],
        out_specs=vmem,
    )(total)


def solution(mesh):
    placed = (
        P(("pgroup", "tile"), None, None),
        P("tile", "pgroup"),
        P("tile", "pgroup"),
        P(None, "tile", None),
        P(),
    )
    return jax.shard_map(
        per_device, mesh=mesh, in_specs=placed, out_specs=P(None, "pgroup", "tile"), check_vma=False
    )
```

```python
import functools

import jax
import jax.numpy as jnp
from jax import lax
from jax.experimental import pallas as pl
from jax.experimental.pallas import tpu as pltpu
from jax.sharding import PartitionSpec as P

MESH = pl.DeviceIdType.MESH
LANES = 128
STEPS = 4
TAPS = 8
TILES = 64
XS = 4
PULSES = 64
COLS = 256
WIDE = 2 * PULSES
SLOTS = STEPS * XS
PIECES = 4
LEG = 32
QUARTERS = 8
QROWS = 64
BUSY = 3
LENT = 6
ROW_BLOCKS = 16
BLOCKS_IN = 32
SIN = (6.2831853, -41.3417004, 81.6051314, -76.7030154, 42.025927, -14.8998467, 3.23813751)
COS = (1, -19.7392087, 64.9393891, -85.4566583, 60.2421313, -26.4046682, 7.80013142, -1.45311229)


def build_profile(echo_ref, table_ref, out_ref, d, part):
    lane = lax.broadcasted_iota(jnp.int32, (16, LANES), 1)
    trow = pl.multiple_of(d * PULSES + part * 16, 16)
    table = table_ref[pl.ds(trow, 16), :]
    first = jnp.broadcast_to(table[:, TAPS : TAPS + 1], (16, LANES)).astype(jnp.int32)
    weights = [jnp.broadcast_to(table[:, j : 1 + j], (16, LANES)) for j in range(TAPS)]
    fine = first & (LANES - 1)
    ahead = lane + fine
    index = ahead & (LANES - 1)
    inside = ahead < LANES
    bits = []
    for level in range(4):
        on = (first >> (7 + level)) & 1
        bits.append(on.astype(jnp.float32).astype(jnp.bfloat16) > 0.5)
    for q in range(2):
        row = pl.multiple_of(q * PULSES + part * 16, 16)
        memo = {}

        def once(f, memo=memo):
            def g(*key):
                k = (f.__name__,) + key
                if k not in memo:
                    memo[k] = f(*key)
                return memo[k]

            return g

        @once
        def loaded(s, row=row):
            s = min(s, BLOCKS_IN - 1)
            return echo_ref[pl.ds(row, 16), s * LANES : (s + 1) * LANES]

        @once
        def chosen(level, s):
            if level == 4:
                return loaded(s)
            return jnp.where(bits[level], chosen(level + 1, s + (1 << level)), chosen(level + 1, s))

        @once
        def turned(s):
            return jnp.take_along_axis(chosen(0, s).astype(jnp.float32), index, axis=1)

        @once
        def window(s):
            return jnp.where(inside, turned(s), turned(s + 1))

        @once
        def rolled(name, s, by):
            return pltpu.roll(makers[name](s), LANES - by, 1)

        def moved(name, s, by):
            if s == ROW_BLOCKS:
                return rolled(name, s, by)
            return jnp.where(lane < LANES - by, rolled(name, s, by), rolled(name, s + 1, by))

        @once
        def next_one(s):
            return moved("w", s, 1)

        @once
        def pair(m, s):
            return weights[2 * m] * window(s) + weights[2 * m + 1] * next_one(s)

        @once
        def quad(m, s):
            return pair(2 * m, s) + moved("p%d" % (2 * m + 1), s, 2)

        makers = {
            "w": window,
            "p1": functools.partial(pair, 1),
            "p3": functools.partial(pair, 3),
            "q1": functools.partial(quad, 1),
        }
        for s in range(ROW_BLOCKS):
            value = quad(0, s) + moved("q1", s, 4)
            out_ref[d * ROW_BLOCKS + s, pl.ds(row, 16), :] = value.astype(jnp.bfloat16)


def half_row(ref, block, *lead):
    at = pl.ds(pl.multiple_of((block >> 1) * LANES, LANES), LANES)
    row = ref[(*lead, slice(None), at)] if lead else ref[:, at]
    return jnp.where((block & 1) == 1, pltpu.roll(row, PULSES, 1), row)


def tables(rates, curves, phase):
    v = lax.broadcasted_iota(jnp.int32, (COLS, LANES), 0).astype(jnp.float32) - (COLS - 1) / 2.0
    turns = rates * v + curves * (v * v * (1.0 / COLS)) + phase
    whole = (turns + 12582912.0) - 12582912.0
    f = turns - whole
    z = f * f
    s = SIN[-1]
    for k in SIN[-2::-1]:
        s = s * z + k
    s = s * f
    c = COS[-1]
    for k in COS[-2::-1]:
        c = c * z + k
    return c.astype(jnp.bfloat16), s.astype(jnp.bfloat16)


def strip_kernel(
    scale, echo_ref, offs_ref, phase_ref, steer_ref, kern_ref, out_ref,
    prof, tab, tsend, kpad, held, left, zsend, relay, zheld, lent, own, tssem, trsem, ssem, rsem, zssem, zrsem, fssem, frsem,
):
    t = lax.axis_index("tile")
    g = lax.axis_index("pgroup")
    x = g >> 1
    zh = g & 1
    here = zh * TILES + t

    def place(n, sign):
        d = n >> 2
        rel = n & (XS - 1)
        other = (here + sign * d) & (2 * TILES - 1)
        return other & (TILES - 1), ((x + sign * rel) & (XS - 1)) * 2 + (other >> 6), other >> 6

    barrier = pltpu.get_barrier_semaphore()

    def greet(n, carry):
        pt, pg, _ = place(n, -1)
        pl.semaphore_signal(barrier, inc=1, device_id=(pt, pg), device_id_type=MESH)
        return carry

    lax.fori_loop(1, SLOTS, greet, 0)
    def along(by):
        other = (here + by) & (2 * TILES - 1)
        return other & (TILES - 1), x * 2 + (other >> 6)

    y = (t >> 1) & 3
    for by in (-LEG, LEG):
        pl.semaphore_signal(barrier, inc=1, device_id=along(by), device_id_type=MESH)

    @pl.when(y == BUSY)
    def _():
        for column in range(BUSY):
            pl.semaphore_signal(
                barrier, inc=1, device_id=along(LEG + (column - BUSY) * 2), device_id_type=MESH
            )

    @pl.when(y != BUSY)
    def _():
        pl.semaphore_signal(barrier, inc=1, device_id=along(LEG + (BUSY - y) * 2), device_id_type=MESH)

    for d in range(1, STEPS):
        pl.semaphore_signal(barrier, inc=1, device_id=((t + d) & (TILES - 1), g), device_id_type=MESH)

    kpad[...] = jnp.zeros_like(kpad)
    kpad[0:TAPS, 0 : kern_ref.shape[1]] = kern_ref[...]
    lane = lax.broadcasted_iota(jnp.int32, (PULSES, LANES), 1)
    eye = lane == lax.broadcasted_iota(jnp.int32, (PULSES, LANES), 0)

    def window_table(d):
        block = (t - d) & (TILES - 1)
        firsts = half_row(offs_ref, block).astype(jnp.float32)
        phases = half_row(phase_ref, block).astype(jnp.float32)
        first = jnp.sum(jnp.where(eye, firsts, 0.0), axis=1, keepdims=True)
        kind = jnp.sum(jnp.where(eye, phases, 0.0), axis=1, keepdims=True)
        onehot = jnp.where(lane.astype(jnp.float32) == kind, 1.0, 0.0)
        weights = lax.dot_general(
            onehot,
            kpad[...],
            (((1,), (1,)), ((), ())),
            precision=lax.Precision.HIGHEST,
            preferred_element_type=jnp.float32,
        )
        return jnp.where(lane == TAPS, first, weights)

    tab[0:PULSES] = window_table(0)
    for d in range(1, STEPS):
        tsend[d - 1] = window_table(d)

    def table_copy(d):
        return pltpu.make_async_remote_copy(
            src_ref=tsend.at[d - 1],
            dst_ref=tab.at[pl.ds(pl.multiple_of(d * PULSES, PULSES), PULSES)],
            send_sem=tssem.at[d],
            recv_sem=trsem.at[d],
            device_id=((t - d) & (TILES - 1), g),
            device_id_type=MESH,
        )

    lane_row = lax.broadcasted_iota(jnp.int32, (1, LANES), 1)
    quarter = jnp.where(lane_row < PULSES, 0.0, 0.25)

    def steer(n, carry):
        d = n >> 2
        rel = n & (XS - 1)
        source = (here - d) & (2 * TILES - 1)
        line = (((x - rel) & (XS - 1)) * 2 + (source >> 6)) * TILES + (source & (TILES - 1))

        def both(i):
            row = half_row(steer_ref, line, i)
            return jnp.where(lane_row < PULSES, row, pltpu.roll(row, PULSES, 1)) * (0.5 / 3.141592653589793)

        re, im = tables(both(0), both(1), quarter)
        at = pl.ds(pl.multiple_of(n * WIDE, WIDE), WIDE)
        left[0:COLS, at] = re
        left[COLS : 2 * COLS, at] = im
        return carry


    def chunk(j, px, ph):
        return px * 4 + (ph ^ 1 ^ (j >> 1)) * 2 + (j & 1)

    def send(j, n):
        pt, pg, ph = place(n, 1)
        return pltpu.make_async_remote_copy(
            src_ref=prof.at[(n >> 2) * ROW_BLOCKS + chunk(j, pg >> 1, ph)],
            dst_ref=held.at[j, pl.ds(pl.multiple_of(n * WIDE, WIDE), WIDE)],
            send_sem=ssem.at[j, n],
            recv_sem=rsem.at[j, n],
            device_id=(pt, pg),
            device_id_type=MESH,
        )

    def distance(i, carry):
        d = (STEPS - i) & (STEPS - 1)

        @pl.when(d > 0)
        def _():
            table_copy(d).wait_recv()

        def part(p, c):
            build_profile(echo_ref, tab, prof, d, p)
            return c

        lax.fori_loop(0, PULSES // 16, part, 0)

        @pl.when(d == 0)
        def _():
            pl.semaphore_wait(barrier, SLOTS + STEPS + jnp.where(y == BUSY, BUSY, 1))
            for b in range(1, STEPS):
                table_copy(b).start()

        def early(j, c):
            for rel in range(XS):
                n = d * XS + rel
                if rel == 0:

                    @pl.when(d > 0)
                    def _():
                        send(j, n).start()

                else:
                    send(j, n).start()
            return c

        lax.fori_loop(0, 2, early, 0)
        return carry

    lax.fori_loop(0, STEPS, distance, 0)

    def late(n, carry):
        send(2, n).start()
        send(3, n).start()
        return carry

    def early_drain(n, carry):
        send(0, n).wait_send()
        send(1, n).wait_send()
        return carry

    lax.fori_loop(0, SLOTS, steer, 0)
    lax.fori_loop(1, SLOTS, early_drain, 0)
    lax.fori_loop(1, SLOTS, late, 0)

    def take(j, carry):
        held[j, 0:WIDE, :] = prof[chunk(j, x, zh)]
        return carry

    lax.fori_loop(0, PIECES, take, 0)

    def arrived(j):
        def one(n, carry):
            send(j, n).wait_recv()
            return carry

        lax.fori_loop(1, SLOTS, one, 0)
        return jnp.dot(left[...], held[j], preferred_element_type=jnp.float32)

    def rows_of(k):
        return pl.ds(pl.multiple_of(k * QROWS, QROWS), QROWS)

    def leg(j, k, second):
        up = jnp.logical_and(k < QUARTERS // 2, y != BUSY)
        return pltpu.make_async_remote_copy(
            src_ref=(relay if second else zsend).at[j, rows_of(k)],
            dst_ref=(zheld if second else relay).at[j, rows_of(k)],
            send_sem=zssem.at[second, j, k],
            recv_sem=zrsem.at[second, j, k],
            device_id=along(jnp.where(up, LEG, -LEG)),
            device_id_type=MESH,
        )

    def lend(j, k):
        return pltpu.make_async_remote_copy(
            src_ref=zsend.at[j, rows_of(k)],
            dst_ref=lent.at[j, k & 1],
            send_sem=zssem.at[0, j, k],
            recv_sem=frsem.at[j, k & 1],
            device_id=along(-LEG + ((k >> 1) - BUSY) * 2),
            device_id_type=MESH,
        )

    def give(j, i):
        return pltpu.make_async_remote_copy(
            src_ref=lent.at[j, i],
            dst_ref=zheld.at[j, rows_of(2 * y + i)],
            send_sem=fssem.at[j, i],
            recv_sem=zrsem.at[1, j, 2 * y + i],
            device_id=along(-LEG + (BUSY - y) * 2),
            device_id_type=MESH,
        )

    def far(j, carry):
        zsend[j] = arrived(j).astype(jnp.bfloat16)

        @pl.when(y == BUSY)
        def _():
            for k in range(LENT):
                lend(j, k).start()

        @pl.when(y != BUSY)
        def _():
            for k in range(LENT):
                leg(j, k, 0).start()

        for k in range(LENT, QUARTERS):
            leg(j, k, 0).start()
        return carry

    def forward(j, carry):
        def on(k):
            leg(j, k, 0).wait_recv()
            leg(j, k, 1).start()

        for k in range(LENT, QUARTERS):
            on(k)

        @pl.when(y != BUSY)
        def _():
            for k in range(LENT):
                on(k)
            for i in range(2):
                lend(j, i).wait_recv()
                give(j, i).start()

        return carry

    def near(j, carry):
        own[j] = arrived(j + 2)
        return carry

    def finish(j, carry):
        for k in range(QUARTERS):
            leg(j, k, 1).wait_recv()
        out_ref[j] = (own[j] + zheld[j].astype(jnp.float32)) * scale
        return carry

    def late_drain(n, carry):
        send(2, n).wait_send()
        send(3, n).wait_send()
        return carry

    lax.fori_loop(0, 2, far, 0)
    lax.fori_loop(0, 2, forward, 0)
    lax.fori_loop(0, 2, near, 0)
    lax.fori_loop(0, 2, finish, 0)
    lax.fori_loop(1, SLOTS, late_drain, 0)
    for d in range(1, STEPS):
        table_copy(d).wait_send()
    for j in range(2):
        for k in range(QUARTERS):
            leg(j, k, 0).wait_send()
        for k in range(LENT, QUARTERS):
            leg(j, k, 1).wait_send()

        @pl.when(y != BUSY)
        def _():
            for k in range(LENT):
                leg(j, k, 1).wait_send()
            for i in range(2):
                give(j, i).wait_send()


def turn_kernel(in_ref, out_ref):
    for j in range(2):
        for i in range(2):
            out_ref[i, j * LANES : (j + 1) * LANES, :] = in_ref[j, i * COLS : (i + 1) * COLS].T


def per_device(echoes, offsets, phase_index, steering, kernels):
    scale = (STEPS * PULSES * lax.axis_size("pgroup")) ** (-0.5)
    vmem = pl.BlockSpec(memory_space=pltpu.VMEM)
    rows = jnp.transpose(echoes, (1, 0, 2)).reshape(WIDE, echoes.shape[2])
    dma = pltpu.SemaphoreType.DMA
    total = pl.pallas_call(
        functools.partial(strip_kernel, scale),
        out_shape=jax.ShapeDtypeStruct((2, 2 * COLS, LANES), jnp.float32),
        in_specs=[vmem] * 5,
        out_specs=vmem,
        scratch_shapes=[
            pltpu.VMEM((STEPS * ROW_BLOCKS, WIDE, LANES), jnp.bfloat16),
            pltpu.VMEM((STEPS * PULSES, LANES), jnp.float32),
            pltpu.VMEM((STEPS - 1, PULSES, LANES), jnp.float32),
            pltpu.VMEM((LANES, LANES), jnp.float32),
            pltpu.VMEM((PIECES, SLOTS * WIDE, LANES), jnp.bfloat16),
            pltpu.VMEM((2 * COLS, SLOTS * WIDE), jnp.bfloat16),
            pltpu.VMEM((2, 2 * COLS, LANES), jnp.bfloat16),
            pltpu.VMEM((2, 2 * COLS, LANES), jnp.bfloat16),
            pltpu.VMEM((2, 2 * COLS, LANES), jnp.bfloat16),
            pltpu.VMEM((2, 2, QROWS, LANES), jnp.bfloat16),
            pltpu.VMEM((2, 2 * COLS, LANES), jnp.float32),
            dma((STEPS,)),
            dma((STEPS,)),
            dma((PIECES, SLOTS)),
            dma((PIECES, SLOTS)),
            dma((2, 2, QUARTERS)),
            dma((2, 2, QUARTERS)),
            dma((2, 2)),
            dma((2, 2)),
        ],
        compiler_params=pltpu.CompilerParams(collective_id=0, has_side_effects=True),
    )(rows, offsets, phase_index, steering, kernels.T)
    return pl.pallas_call(
        turn_kernel,
        out_shape=jax.ShapeDtypeStruct((2, COLS, COLS), jnp.float32),
        in_specs=[vmem],
        out_specs=vmem,
    )(total)


def solution(mesh):
    placed = (
        P(("pgroup", "tile"), None, None),
        P("tile", "pgroup"),
        P("tile", "pgroup"),
        P(None, "tile", None),
        P(),
    )
    return jax.shard_map(
        per_device, mesh=mesh, in_specs=placed, out_specs=P(None, "pgroup", "tile"), check_vma=False
    )
```

```python
import functools

import jax
import jax.numpy as jnp
from jax import lax
from jax.experimental import pallas as pl
from jax.experimental.pallas import tpu as pltpu
from jax.sharding import PartitionSpec as P

MESH = pl.DeviceIdType.MESH
LANES = 128
STEPS = 4
TAPS = 8
TILES = 64
XS = 4
PULSES = 64
COLS = 256
WIDE = 2 * PULSES
SLOTS = STEPS * XS
PIECES = 4
LEG = 32
QUARTERS = 8
QROWS = 64
BUSY = 3
LENT = 6
ROW_BLOCKS = 16
BLOCKS_IN = 32
SIN = (6.2831853, -41.3417004, 81.6051314, -76.7030154, 42.025927, -14.8998467, 3.23813751)
COS = (1, -19.7392087, 64.9393891, -85.4566583, 60.2421313, -26.4046682, 7.80013142, -1.45311229)


def build_profile(echo_ref, table_ref, out_ref, d, part):
    lane = lax.broadcasted_iota(jnp.int32, (16, LANES), 1)
    trow = pl.multiple_of(d * PULSES + part * 16, 16)
    table = table_ref[pl.ds(trow, 16), :]
    first = jnp.broadcast_to(table[:, TAPS : TAPS + 1], (16, LANES)).astype(jnp.int32)
    weights = [jnp.broadcast_to(table[:, j : 1 + j], (16, LANES)) for j in range(TAPS)]
    fine = first & (LANES - 1)
    ahead = lane + fine
    index = ahead & (LANES - 1)
    inside = ahead < LANES
    bits = []
    for level in range(4):
        on = (first >> (7 + level)) & 1
        bits.append(on.astype(jnp.float32).astype(jnp.bfloat16) > 0.5)
    for q in range(2):
        row = pl.multiple_of(q * PULSES + part * 16, 16)
        memo = {}

        def once(f, memo=memo):
            def g(*key):
                k = (f.__name__,) + key
                if k not in memo:
                    memo[k] = f(*key)
                return memo[k]

            return g

        @once
        def loaded(s, row=row):
            s = min(s, BLOCKS_IN - 1)
            return echo_ref[pl.ds(row, 16), s * LANES : (s + 1) * LANES]

        @once
        def chosen(level, s):
            if level == 4:
                return loaded(s)
            return jnp.where(bits[level], chosen(level + 1, s + (1 << level)), chosen(level + 1, s))

        @once
        def turned(s):
            return jnp.take_along_axis(chosen(0, s).astype(jnp.float32), index, axis=1)

        @once
        def window(s):
            return jnp.where(inside, turned(s), turned(s + 1))

        @once
        def rolled(name, s, by):
            return pltpu.roll(makers[name](s), LANES - by, 1)

        def moved(name, s, by):
            if s == ROW_BLOCKS:
                return rolled(name, s, by)
            return jnp.where(lane < LANES - by, rolled(name, s, by), rolled(name, s + 1, by))

        @once
        def next_one(s):
            return moved("w", s, 1)

        @once
        def pair(m, s):
            return weights[2 * m] * window(s) + weights[2 * m + 1] * next_one(s)

        @once
        def quad(m, s):
            return pair(2 * m, s) + moved("p%d" % (2 * m + 1), s, 2)

        makers = {
            "w": window,
            "p1": functools.partial(pair, 1),
            "p3": functools.partial(pair, 3),
            "q1": functools.partial(quad, 1),
        }
        for s in range(ROW_BLOCKS):
            value = quad(0, s) + moved("q1", s, 4)
            out_ref[d * ROW_BLOCKS + s, pl.ds(row, 16), :] = value.astype(jnp.bfloat16)


def half_row(ref, block, *lead):
    at = pl.ds(pl.multiple_of((block >> 1) * LANES, LANES), LANES)
    row = ref[(*lead, slice(None), at)] if lead else ref[:, at]
    return jnp.where((block & 1) == 1, pltpu.roll(row, PULSES, 1), row)


def tables(rates, curves, phase):
    v = lax.broadcasted_iota(jnp.int32, (COLS, LANES), 0).astype(jnp.float32) - (COLS - 1) / 2.0
    turns = rates * v + curves * (v * v * (1.0 / COLS)) + phase
    whole = (turns + 12582912.0) - 12582912.0
    f = turns - whole
    z = f * f
    s = SIN[-1]
    for k in SIN[-2::-1]:
        s = s * z + k
    s = s * f
    c = COS[-1]
    for k in COS[-2::-1]:
        c = c * z + k
    return c.astype(jnp.bfloat16), s.astype(jnp.bfloat16)


def strip_kernel(
    scale, echo_ref, offs_ref, phase_ref, steer_ref, kern_ref, out_ref,
    prof, tab, tsend, kpad, held, left, zsend, relay, zheld, lent, own, tssem, trsem, ssem, rsem, zssem, zrsem, fssem, frsem,
):
    t = lax.axis_index("tile")
    g = lax.axis_index("pgroup")
    x = g >> 1
    zh = g & 1
    here = zh * TILES + t

    def place(n, sign):
        d = n >> 2
        rel = n & (XS - 1)
        other = (here + sign * d) & (2 * TILES - 1)
        return other & (TILES - 1), ((x + sign * rel) & (XS - 1)) * 2 + (other >> 6), other >> 6

    barrier = pltpu.get_barrier_semaphore()

    def greet(n, carry):
        pt, pg, _ = place(n, -1)
        pl.semaphore_signal(barrier, inc=1, device_id=(pt, pg), device_id_type=MESH)
        return carry

    lax.fori_loop(1, SLOTS, greet, 0)
    def along(by):
        other = (here + by) & (2 * TILES - 1)
        return other & (TILES - 1), x * 2 + (other >> 6)

    y = (t >> 1) & 3
    for by in (-LEG, LEG):
        pl.semaphore_signal(barrier, inc=1, device_id=along(by), device_id_type=MESH)

    @pl.when(y == BUSY)
    def _():
        for column in range(BUSY):
            pl.semaphore_signal(
                barrier, inc=1, device_id=along(LEG + (column - BUSY) * 2), device_id_type=MESH
            )

    @pl.when(y != BUSY)
    def _():
        pl.semaphore_signal(barrier, inc=1, device_id=along(LEG + (BUSY - y) * 2), device_id_type=MESH)

    for d in range(1, STEPS):
        pl.semaphore_signal(barrier, inc=1, device_id=((t + d) & (TILES - 1), g), device_id_type=MESH)

    kpad[...] = jnp.zeros_like(kpad)
    kpad[0:TAPS, 0 : kern_ref.shape[1]] = kern_ref[...]
    lane = lax.broadcasted_iota(jnp.int32, (PULSES, LANES), 1)
    eye = lane == lax.broadcasted_iota(jnp.int32, (PULSES, LANES), 0)

    def window_table(d):
        block = (t - d) & (TILES - 1)
        firsts = half_row(offs_ref, block).astype(jnp.float32)
        phases = half_row(phase_ref, block).astype(jnp.float32)
        first = jnp.sum(jnp.where(eye, firsts, 0.0), axis=1, keepdims=True)
        kind = jnp.sum(jnp.where(eye, phases, 0.0), axis=1, keepdims=True)
        onehot = jnp.where(lane.astype(jnp.float32) == kind, 1.0, 0.0)
        weights = lax.dot_general(
            onehot,
            kpad[...],
            (((1,), (1,)), ((), ())),
            precision=lax.Precision.HIGHEST,
            preferred_element_type=jnp.float32,
        )
        return jnp.where(lane == TAPS, first, weights)

    tab[0:PULSES] = window_table(0)
    for d in range(1, STEPS):
        tsend[d - 1] = window_table(d)

    def table_copy(d):
        return pltpu.make_async_remote_copy(
            src_ref=tsend.at[d - 1],
            dst_ref=tab.at[pl.ds(pl.multiple_of(d * PULSES, PULSES), PULSES)],
            send_sem=tssem.at[d],
            recv_sem=trsem.at[d],
            device_id=((t - d) & (TILES - 1), g),
            device_id_type=MESH,
        )

    lane_row = lax.broadcasted_iota(jnp.int32, (1, LANES), 1)
    quarter = jnp.where(lane_row < PULSES, 0.0, 0.25)

    def steer(n, carry):
        d = n >> 2
        rel = n & (XS - 1)
        source = (here - d) & (2 * TILES - 1)
        line = (((x - rel) & (XS - 1)) * 2 + (source >> 6)) * TILES + (source & (TILES - 1))

        def both(i):
            row = half_row(steer_ref, line, i)
            return jnp.where(lane_row < PULSES, row, pltpu.roll(row, PULSES, 1)) * (0.5 / 3.141592653589793)

        re, im = tables(both(0), both(1), quarter)
        at = pl.ds(pl.multiple_of(n * WIDE, WIDE), WIDE)
        left[0:COLS, at] = re
        left[COLS : 2 * COLS, at] = im
        return carry


    def chunk(j, px, ph):
        return px * 4 + (ph ^ 1 ^ (j >> 1)) * 2 + (j & 1)

    def send(j, n):
        pt, pg, ph = place(n, 1)
        return pltpu.make_async_remote_copy(
            src_ref=prof.at[(n >> 2) * ROW_BLOCKS + chunk(j, pg >> 1, ph)],
            dst_ref=held.at[j, pl.ds(pl.multiple_of(n * WIDE, WIDE), WIDE)],
            send_sem=ssem.at[j, n],
            recv_sem=rsem.at[j, n],
            device_id=(pt, pg),
            device_id_type=MESH,
        )

    first_slots = jnp.where(t > TILES - STEPS, SLOTS, SLOTS // 2)

    def distance(i, carry):
        d = i

        @pl.when(d > 0)
        def _():
            table_copy(d).wait_recv()

        def part(p, c):
            build_profile(echo_ref, tab, prof, d, p)
            return c

        lax.fori_loop(0, PULSES // 16, part, 0)

        @pl.when(d == 0)
        def _():
            pl.semaphore_wait(barrier, SLOTS + STEPS + jnp.where(y == BUSY, BUSY, 1))
            for b in range(1, STEPS):
                table_copy(b).start()

        @pl.when(d > 0)
        def _():
            send(0, d * XS).start()

        for rel in range(1, XS):
            send(0, d * XS + rel).start()

        @pl.when(d == 0)
        def _():
            lax.fori_loop(0, first_slots, steer, 0)

        return carry

    lax.fori_loop(0, STEPS, distance, 0)

    def second(n, carry):
        send(1, n).start()
        return carry

    def late(n, carry):
        send(2, n).start()
        send(3, n).start()
        return carry

    def early_drain(n, carry):
        send(0, n).wait_send()
        send(1, n).wait_send()
        return carry

    lax.fori_loop(1, SLOTS, second, 0)
    lax.fori_loop(first_slots, SLOTS, steer, 0)

    def take(j, carry):
        held[j, 0:WIDE, :] = prof[chunk(j, x, zh)]
        return carry

    lax.fori_loop(0, PIECES, take, 0)

    def arrived(j):
        def one(n, carry):
            send(j, n).wait_recv()
            return carry

        lax.fori_loop(1, SLOTS, one, 0)
        return jnp.dot(left[...], held[j], preferred_element_type=jnp.float32)

    def rows_of(k):
        return pl.ds(pl.multiple_of(k * QROWS, QROWS), QROWS)

    def leg(j, k, second):
        up = jnp.logical_and(k < QUARTERS // 2, y != BUSY)
        return pltpu.make_async_remote_copy(
            src_ref=(relay if second else zsend).at[j, rows_of(k)],
            dst_ref=(zheld if second else relay).at[j, rows_of(k)],
            send_sem=zssem.at[second, j, k],
            recv_sem=zrsem.at[second, j, k],
            device_id=along(jnp.where(up, LEG, -LEG)),
            device_id_type=MESH,
        )

    def lend(j, k):
        return pltpu.make_async_remote_copy(
            src_ref=zsend.at[j, rows_of(k)],
            dst_ref=lent.at[j, k & 1],
            send_sem=zssem.at[0, j, k],
            recv_sem=frsem.at[j, k & 1],
            device_id=along(-LEG + ((k >> 1) - BUSY) * 2),
            device_id_type=MESH,
        )

    def give(j, i):
        return pltpu.make_async_remote_copy(
            src_ref=lent.at[j, i],
            dst_ref=zheld.at[j, rows_of(2 * y + i)],
            send_sem=fssem.at[j, i],
            recv_sem=zrsem.at[1, j, 2 * y + i],
            device_id=along(-LEG + (BUSY - y) * 2),
            device_id_type=MESH,
        )

    def far(j, carry):
        zsend[j] = arrived(j).astype(jnp.bfloat16)

        @pl.when(y == BUSY)
        def _():
            for k in range(LENT):
                lend(j, k).start()

        @pl.when(y != BUSY)
        def _():
            for k in range(LENT):
                leg(j, k, 0).start()

        for k in range(LENT, QUARTERS):
            leg(j, k, 0).start()
        return carry

    def forward(j, carry):
        def on(k):
            leg(j, k, 0).wait_recv()
            leg(j, k, 1).start()

        for k in range(LENT, QUARTERS):
            on(k)

        @pl.when(y != BUSY)
        def _():
            for k in range(LENT):
                on(k)
            for i in range(2):
                lend(j, i).wait_recv()
                give(j, i).start()

        return carry

    def near(j, carry):
        own[j] = arrived(j + 2)
        return carry

    def finish(j, carry):
        for k in range(QUARTERS):
            leg(j, k, 1).wait_recv()
        out_ref[j] = (own[j] + zheld[j].astype(jnp.float32)) * scale
        return carry

    def late_drain(n, carry):
        send(2, n).wait_send()
        send(3, n).wait_send()
        return carry

    far(0, 0)
    lax.fori_loop(1, SLOTS, early_drain, 0)
    lax.fori_loop(1, SLOTS, late, 0)
    far(1, 0)
    lax.fori_loop(0, 2, forward, 0)
    lax.fori_loop(0, 2, near, 0)
    lax.fori_loop(0, 2, finish, 0)
    lax.fori_loop(1, SLOTS, late_drain, 0)
    for d in range(1, STEPS):
        table_copy(d).wait_send()
    for j in range(2):
        for k in range(QUARTERS):
            leg(j, k, 0).wait_send()
        for k in range(LENT, QUARTERS):
            leg(j, k, 1).wait_send()

        @pl.when(y != BUSY)
        def _():
            for k in range(LENT):
                leg(j, k, 1).wait_send()
            for i in range(2):
                give(j, i).wait_send()


def turn_kernel(in_ref, out_ref):
    for j in range(2):
        for i in range(2):
            out_ref[i, j * LANES : (j + 1) * LANES, :] = in_ref[j, i * COLS : (i + 1) * COLS].T


def per_device(echoes, offsets, phase_index, steering, kernels):
    scale = (STEPS * PULSES * lax.axis_size("pgroup")) ** (-0.5)
    vmem = pl.BlockSpec(memory_space=pltpu.VMEM)
    rows = jnp.transpose(echoes, (1, 0, 2)).reshape(WIDE, echoes.shape[2])
    dma = pltpu.SemaphoreType.DMA
    total = pl.pallas_call(
        functools.partial(strip_kernel, scale),
        out_shape=jax.ShapeDtypeStruct((2, 2 * COLS, LANES), jnp.float32),
        in_specs=[vmem] * 5,
        out_specs=vmem,
        scratch_shapes=[
            pltpu.VMEM((STEPS * ROW_BLOCKS, WIDE, LANES), jnp.bfloat16),
            pltpu.VMEM((STEPS * PULSES, LANES), jnp.float32),
            pltpu.VMEM((STEPS - 1, PULSES, LANES), jnp.float32),
            pltpu.VMEM((LANES, LANES), jnp.float32),
            pltpu.VMEM((PIECES, SLOTS * WIDE, LANES), jnp.bfloat16),
            pltpu.VMEM((2 * COLS, SLOTS * WIDE), jnp.bfloat16),
            pltpu.VMEM((2, 2 * COLS, LANES), jnp.bfloat16),
            pltpu.VMEM((2, 2 * COLS, LANES), jnp.bfloat16),
            pltpu.VMEM((2, 2 * COLS, LANES), jnp.bfloat16),
            pltpu.VMEM((2, 2, QROWS, LANES), jnp.bfloat16),
            pltpu.VMEM((2, 2 * COLS, LANES), jnp.float32),
            dma((STEPS,)),
            dma((STEPS,)),
            dma((PIECES, SLOTS)),
            dma((PIECES, SLOTS)),
            dma((2, 2, QUARTERS)),
            dma((2, 2, QUARTERS)),
            dma((2, 2)),
            dma((2, 2)),
        ],
        compiler_params=pltpu.CompilerParams(collective_id=0, has_side_effects=True),
    )(rows, offsets, phase_index, steering, kernels.T)
    return pl.pallas_call(
        turn_kernel,
        out_shape=jax.ShapeDtypeStruct((2, COLS, COLS), jnp.float32),
        in_specs=[vmem],
        out_specs=vmem,
    )(total)


def solution(mesh):
    placed = (
        P(("pgroup", "tile"), None, None),
        P("tile", "pgroup"),
        P("tile", "pgroup"),
        P(None, "tile", None),
        P(),
    )
    return jax.shard_map(
        per_device, mesh=mesh, in_specs=placed, out_specs=P(None, "pgroup", "tile"), check_vma=False
    )
```

```python
import functools

import jax
import jax.numpy as jnp
from jax import lax
from jax.experimental import pallas as pl
from jax.experimental.pallas import tpu as pltpu
from jax.sharding import PartitionSpec as P

MESH = pl.DeviceIdType.MESH
LANES = 128
STEPS = 4
TAPS = 8
TILES = 64
XS = 4
PULSES = 64
COLS = 256
WIDE = 2 * PULSES
SLOTS = STEPS * XS
PIECES = 4
LEG = 32
QUARTERS = 8
QROWS = 64
BUSY = 3
LENT = 6
ROW_BLOCKS = 16
BLOCKS_IN = 32
SIN = (6.2831853, -41.3417004, 81.6051314, -76.7030154, 42.025927, -14.8998467, 3.23813751)
COS = (1, -19.7392087, 64.9393891, -85.4566583, 60.2421313, -26.4046682, 7.80013142, -1.45311229)


def build_profile(echo_ref, table_ref, out_ref, d, part):
    lane = lax.broadcasted_iota(jnp.int32, (16, LANES), 1)
    trow = pl.multiple_of(d * PULSES + part * 16, 16)
    table = table_ref[pl.ds(trow, 16), :]
    first = jnp.broadcast_to(table[:, TAPS : TAPS + 1], (16, LANES)).astype(jnp.int32)
    weights = [jnp.broadcast_to(table[:, j : 1 + j], (16, LANES)) for j in range(TAPS)]
    fine = first & (LANES - 1)
    ahead = lane + fine
    index = ahead & (LANES - 1)
    inside = ahead < LANES
    bits = []
    for level in range(4):
        on = (first >> (7 + level)) & 1
        bits.append(on.astype(jnp.float32).astype(jnp.bfloat16) > 0.5)
    for q in range(2):
        row = pl.multiple_of(q * PULSES + part * 16, 16)
        memo = {}

        def once(f, memo=memo):
            def g(*key):
                k = (f.__name__,) + key
                if k not in memo:
                    memo[k] = f(*key)
                return memo[k]

            return g

        @once
        def loaded(s, row=row):
            s = min(s, BLOCKS_IN - 1)
            return echo_ref[pl.ds(row, 16), s * LANES : (s + 1) * LANES]

        @once
        def chosen(level, s):
            if level == 4:
                return loaded(s)
            return jnp.where(bits[level], chosen(level + 1, s + (1 << level)), chosen(level + 1, s))

        @once
        def turned(s):
            return jnp.take_along_axis(chosen(0, s).astype(jnp.float32), index, axis=1)

        @once
        def window(s):
            return jnp.where(inside, turned(s), turned(s + 1))

        @once
        def rolled(name, s, by):
            return pltpu.roll(makers[name](s), LANES - by, 1)

        def moved(name, s, by):
            if s == ROW_BLOCKS:
                return rolled(name, s, by)
            return jnp.where(lane < LANES - by, rolled(name, s, by), rolled(name, s + 1, by))

        @once
        def next_one(s):
            return moved("w", s, 1)

        @once
        def pair(m, s):
            return weights[2 * m] * window(s) + weights[2 * m + 1] * next_one(s)

        @once
        def quad(m, s):
            return pair(2 * m, s) + moved("p%d" % (2 * m + 1), s, 2)

        makers = {
            "w": window,
            "p1": functools.partial(pair, 1),
            "p3": functools.partial(pair, 3),
            "q1": functools.partial(quad, 1),
        }
        for s in range(ROW_BLOCKS):
            value = quad(0, s) + moved("q1", s, 4)
            out_ref[d * ROW_BLOCKS + s, pl.ds(row, 16), :] = value.astype(jnp.bfloat16)


def half_row(ref, block, *lead):
    at = pl.ds(pl.multiple_of((block >> 1) * LANES, LANES), LANES)
    row = ref[(*lead, slice(None), at)] if lead else ref[:, at]
    return jnp.where((block & 1) == 1, pltpu.roll(row, PULSES, 1), row)


def tables(rates, curves, phase):
    v = lax.broadcasted_iota(jnp.int32, (COLS, LANES), 0).astype(jnp.float32) - (COLS - 1) / 2.0
    turns = rates * v + curves * (v * v * (1.0 / COLS)) + phase
    whole = (turns + 12582912.0) - 12582912.0
    f = turns - whole
    z = f * f
    s = SIN[-1]
    for k in SIN[-2::-1]:
        s = s * z + k
    s = s * f
    c = COS[-1]
    for k in COS[-2::-1]:
        c = c * z + k
    return c.astype(jnp.bfloat16), s.astype(jnp.bfloat16)


def strip_kernel(
    scale, echo_ref, offs_ref, phase_ref, steer_ref, kern_ref, out_ref,
    prof, tab, tsend, kpad, held, left, zsend, relay, zheld, lent, own, tssem, trsem, ssem, rsem, zssem, zrsem, fssem, frsem,
):
    t = lax.axis_index("tile")
    g = lax.axis_index("pgroup")
    x = g >> 1
    zh = g & 1
    here = zh * TILES + t

    def place(n, sign):
        d = n >> 2
        rel = n & (XS - 1)
        other = (here + sign * d) & (2 * TILES - 1)
        return other & (TILES - 1), ((x + sign * rel) & (XS - 1)) * 2 + (other >> 6), other >> 6

    barrier = pltpu.get_barrier_semaphore()

    def greet(n, carry):
        pt, pg, _ = place(n, -1)
        pl.semaphore_signal(barrier, inc=1, device_id=(pt, pg), device_id_type=MESH)
        return carry

    lax.fori_loop(1, SLOTS, greet, 0)
    def along(by):
        other = (here + by) & (2 * TILES - 1)
        return other & (TILES - 1), x * 2 + (other >> 6)

    y = (t >> 1) & 3
    for by in (-LEG, LEG):
        pl.semaphore_signal(barrier, inc=1, device_id=along(by), device_id_type=MESH)

    @pl.when(y == BUSY)
    def _():
        for column in range(BUSY):
            pl.semaphore_signal(
                barrier, inc=1, device_id=along(LEG + (column - BUSY) * 2), device_id_type=MESH
            )

    @pl.when(y != BUSY)
    def _():
        pl.semaphore_signal(barrier, inc=1, device_id=along(LEG + (BUSY - y) * 2), device_id_type=MESH)

    for d in range(1, STEPS):
        pl.semaphore_signal(barrier, inc=1, device_id=((t + d) & (TILES - 1), g), device_id_type=MESH)

    kpad[...] = jnp.zeros_like(kpad)
    kpad[0:TAPS, 0 : kern_ref.shape[1]] = kern_ref[...]
    lane = lax.broadcasted_iota(jnp.int32, (PULSES, LANES), 1)
    eye = lane == lax.broadcasted_iota(jnp.int32, (PULSES, LANES), 0)

    def window_table(d):
        block = (t - d) & (TILES - 1)
        firsts = half_row(offs_ref, block).astype(jnp.float32)
        phases = half_row(phase_ref, block).astype(jnp.float32)
        first = jnp.sum(jnp.where(eye, firsts, 0.0), axis=1, keepdims=True)
        kind = jnp.sum(jnp.where(eye, phases, 0.0), axis=1, keepdims=True)
        onehot = jnp.where(lane.astype(jnp.float32) == kind, 1.0, 0.0)
        weights = lax.dot_general(
            onehot,
            kpad[...],
            (((1,), (1,)), ((), ())),
            precision=lax.Precision.HIGHEST,
            preferred_element_type=jnp.float32,
        )
        return jnp.where(lane == TAPS, first, weights)

    tab[0:PULSES] = window_table(0)
    for d in range(1, STEPS):
        tsend[d - 1] = window_table(d)

    def table_copy(d):
        return pltpu.make_async_remote_copy(
            src_ref=tsend.at[d - 1],
            dst_ref=tab.at[pl.ds(pl.multiple_of(d * PULSES, PULSES), PULSES)],
            send_sem=tssem.at[d],
            recv_sem=trsem.at[d],
            device_id=((t - d) & (TILES - 1), g),
            device_id_type=MESH,
        )

    lane_row = lax.broadcasted_iota(jnp.int32, (1, LANES), 1)
    quarter = jnp.where(lane_row < PULSES, 0.0, 0.25)

    def steer(n, carry):
        d = n >> 2
        rel = n & (XS - 1)
        source = (here - d) & (2 * TILES - 1)
        line = (((x - rel) & (XS - 1)) * 2 + (source >> 6)) * TILES + (source & (TILES - 1))

        def both(i):
            row = half_row(steer_ref, line, i)
            return jnp.where(lane_row < PULSES, row, pltpu.roll(row, PULSES, 1)) * (0.5 / 3.141592653589793)

        re, im = tables(both(0), both(1), quarter)
        at = pl.ds(pl.multiple_of(n * WIDE, WIDE), WIDE)
        left[0:COLS, at] = re
        left[COLS : 2 * COLS, at] = im
        return carry


    def chunk(j, px, ph):
        return px * 4 + (ph ^ 1 ^ (j >> 1)) * 2 + (j & 1)

    def send(j, n):
        pt, pg, ph = place(n, 1)
        return pltpu.make_async_remote_copy(
            src_ref=prof.at[(n >> 2) * ROW_BLOCKS + chunk(j, pg >> 1, ph)],
            dst_ref=held.at[j, pl.ds(pl.multiple_of(n * WIDE, WIDE), WIDE)],
            send_sem=ssem.at[j, n],
            recv_sem=rsem.at[j, n],
            device_id=(pt, pg),
            device_id_type=MESH,
        )

    first_slots = jnp.where(t > TILES - STEPS, SLOTS, SLOTS // 2)

    def distance(i, carry):
        d = i

        @pl.when(d > 0)
        def _():
            table_copy(d).wait_recv()

        def part(p, c):
            build_profile(echo_ref, tab, prof, d, p)
            return c

        lax.fori_loop(0, PULSES // 16, part, 0)

        @pl.when(d == 0)
        def _():
            pl.semaphore_wait(barrier, SLOTS + STEPS + jnp.where(y == BUSY, BUSY, 1))
            for b in range(1, STEPS):
                table_copy(b).start()

        @pl.when(d > 0)
        def _():
            send(0, d * XS).start()

        for rel in range(1, XS):
            send(0, d * XS + rel).start()

        @pl.when(d == 0)
        def _():
            lax.fori_loop(0, first_slots, steer, 0)

        return carry

    lax.fori_loop(0, STEPS, distance, 0)

    def second(n, carry):
        send(1, n).start()
        return carry

    def late(n, carry):
        send(2, n).start()
        send(3, n).start()
        return carry

    def early_drain(n, carry):
        send(0, n).wait_send()
        send(1, n).wait_send()
        return carry

    lax.fori_loop(1, SLOTS, second, 0)
    lax.fori_loop(first_slots, SLOTS, steer, 0)

    def take(j, carry):
        held[j, 0:WIDE, :] = prof[chunk(j, x, zh)]
        return carry

    lax.fori_loop(0, PIECES, take, 0)

    def arrived(j):
        def one(n, carry):
            send(j, n).wait_recv()
            return carry

        lax.fori_loop(1, SLOTS, one, 0)
        return jnp.dot(left[...], held[j], preferred_element_type=jnp.float32)

    def rows_of(k):
        return pl.ds(pl.multiple_of(k * QROWS, QROWS), QROWS)

    def leg(j, k, second):
        up = jnp.logical_and(k < QUARTERS // 2, y != BUSY)
        return pltpu.make_async_remote_copy(
            src_ref=(relay if second else zsend).at[j, rows_of(k)],
            dst_ref=(zheld if second else relay).at[j, rows_of(k)],
            send_sem=zssem.at[second, j, k],
            recv_sem=zrsem.at[second, j, k],
            device_id=along(jnp.where(up, LEG, -LEG)),
            device_id_type=MESH,
        )

    def lend(j, k):
        return pltpu.make_async_remote_copy(
            src_ref=zsend.at[j, rows_of(k)],
            dst_ref=lent.at[j, k & 1],
            send_sem=zssem.at[0, j, k],
            recv_sem=frsem.at[j, k & 1],
            device_id=along(-LEG + ((k >> 1) - BUSY) * 2),
            device_id_type=MESH,
        )

    def give(j, i):
        return pltpu.make_async_remote_copy(
            src_ref=lent.at[j, i],
            dst_ref=zheld.at[j, rows_of(2 * y + i)],
            send_sem=fssem.at[j, i],
            recv_sem=zrsem.at[1, j, 2 * y + i],
            device_id=along(-LEG + (BUSY - y) * 2),
            device_id_type=MESH,
        )

    def far(j, carry):
        zsend[j] = arrived(j).astype(jnp.bfloat16)

        @pl.when(y == BUSY)
        def _():
            for k in range(LENT):
                lend(j, k).start()

        @pl.when(y != BUSY)
        def _():
            for k in range(LENT):
                leg(j, k, 0).start()

        for k in range(LENT, QUARTERS):
            leg(j, k, 0).start()
        return carry

    def forward(j, carry):
        def on(k):
            leg(j, k, 0).wait_recv()
            leg(j, k, 1).start()

        for k in range(LENT, QUARTERS):
            on(k)

        @pl.when(y != BUSY)
        def _():
            for k in range(LENT):
                on(k)
            for i in range(2):
                lend(j, i).wait_recv()
                give(j, i).start()

        return carry

    def near(j, carry):
        own[j] = arrived(j + 2)
        return carry

    def finish(j, carry):
        for k in range(QUARTERS):
            leg(j, k, 1).wait_recv()
        out_ref[j] = (own[j] + zheld[j].astype(jnp.float32)) * scale
        return carry

    def late_drain(n, carry):
        send(2, n).wait_send()
        send(3, n).wait_send()
        return carry

    far(0, 0)
    lax.fori_loop(1, SLOTS, early_drain, 0)
    lax.fori_loop(1, SLOTS, late, 0)
    far(1, 0)
    lax.fori_loop(0, 2, forward, 0)
    lax.fori_loop(0, 2, near, 0)
    lax.fori_loop(0, 2, finish, 0)
    lax.fori_loop(1, SLOTS, late_drain, 0)
    for d in range(1, STEPS):
        table_copy(d).wait_send()
    for j in range(2):
        for k in range(QUARTERS):
            leg(j, k, 0).wait_send()
        for k in range(LENT, QUARTERS):
            leg(j, k, 1).wait_send()

        @pl.when(y != BUSY)
        def _():
            for k in range(LENT):
                leg(j, k, 1).wait_send()
            for i in range(2):
                give(j, i).wait_send()


def turn_kernel(in_ref, out_ref):
    for j in range(2):
        for i in range(2):
            out_ref[i, j * LANES : (j + 1) * LANES, :] = in_ref[j, i * COLS : (i + 1) * COLS].T


def per_device(echoes, offsets, phase_index, steering, kernels):
    scale = (STEPS * PULSES * lax.axis_size("pgroup")) ** (-0.5)
    vmem = pl.BlockSpec(memory_space=pltpu.VMEM)
    rows = jnp.transpose(echoes, (1, 0, 2)).reshape(WIDE, echoes.shape[2])
    dma = pltpu.SemaphoreType.DMA
    total = pl.pallas_call(
        functools.partial(strip_kernel, scale),
        out_shape=jax.ShapeDtypeStruct((2, 2 * COLS, LANES), jnp.float32),
        in_specs=[vmem] * 5,
        out_specs=vmem,
        scratch_shapes=[
            pltpu.VMEM((STEPS * ROW_BLOCKS, WIDE, LANES), jnp.bfloat16),
            pltpu.VMEM((STEPS * PULSES, LANES), jnp.float32),
            pltpu.VMEM((STEPS - 1, PULSES, LANES), jnp.float32),
            pltpu.VMEM((LANES, LANES), jnp.float32),
            pltpu.VMEM((PIECES, SLOTS * WIDE, LANES), jnp.bfloat16),
            pltpu.VMEM((2 * COLS, SLOTS * WIDE), jnp.bfloat16),
            pltpu.VMEM((2, 2 * COLS, LANES), jnp.bfloat16),
            pltpu.VMEM((2, 2 * COLS, LANES), jnp.bfloat16),
            pltpu.VMEM((2, 2 * COLS, LANES), jnp.bfloat16),
            pltpu.VMEM((2, 2, QROWS, LANES), jnp.bfloat16),
            pltpu.VMEM((2, 2 * COLS, LANES), jnp.float32),
            dma((STEPS,)),
            dma((STEPS,)),
            dma((PIECES, SLOTS)),
            dma((PIECES, SLOTS)),
            dma((2, 2, QUARTERS)),
            dma((2, 2, QUARTERS)),
            dma((2, 2)),
            dma((2, 2)),
        ],
        compiler_params=pltpu.CompilerParams(
            collective_id=0, has_side_effects=True, vmem_limit_bytes=24 * 1024 * 1024
        ),
    )(rows, offsets, phase_index, steering, kernels.T)
    return pl.pallas_call(
        turn_kernel,
        out_shape=jax.ShapeDtypeStruct((2, COLS, COLS), jnp.float32),
        in_specs=[vmem],
        out_specs=vmem,
        compiler_params=pltpu.CompilerParams(vmem_limit_bytes=8 * 1024 * 1024),
    )(total)


def solution(mesh):
    placed = (
        P(("pgroup", "tile"), None, None),
        P("tile", "pgroup"),
        P("tile", "pgroup"),
        P(None, "tile", None),
        P(),
    )
    return jax.shard_map(
        per_device, mesh=mesh, in_specs=placed, out_specs=P(None, "pgroup", "tile"), check_vma=False
    )
```
